32 devices in a mesh: dp: 8 (over y, x, core), tensor: 4 (over z).
Axes of the slice: x: 2, y: 2, z: 4, core: 2. Of those that a mesh axis runs over, the one named last changes fastest.
Arguments:
- hidden_in: bfloat16 [8192, 2048], P(('dp', 'tensor')), may hold values from -6 to 6
- w_qkv: bfloat16 [2048, 3, 2048], P('dp', None, 'tensor'), may hold values from -0.125 to 0.125
- qv_bias: float32 [2, 2048], P(None, 'tensor'), may hold values from -3 to 3
- k_bias: float32 [32, 16], P('tensor'), may hold values from -3 to 3
- w_out: bfloat16 [2048, 2048], P('dp', 'tensor'), may hold values from -1 to 1
- ln_gain: float32 [2, 2048], replicated, may hold values from 0.5 to 1.5
- ln_bias: float32 [2, 2048], replicated, may hold values from -1.75 to 1.75
- w_gate_up: bfloat16 [2048, 2, 5632], P('dp', None, 'tensor'), may hold values from -0.125 to 0.125
- w_down: bfloat16 [2048, 5632], P('dp', 'tensor'), may hold values from -0.078125 to 0.078125
- cotangent: bfloat16 [8192, 2048], P(('dp', 'tensor')), may hold values from -12 to 12
Outputs:
- layer_out: bfloat16 [8192, 2048], P(('dp', 'tensor'))
- grad_input: bfloat16 [8192, 2048], P(('dp', 'tensor'))
- grad_qkv: float32 [2048, 3, 2048], P('dp', None, 'tensor')
- grad_qv_bias: float32 [2, 2048], P(None, 'tensor')
- grad_k_bias: float32 [32, 16], P('tensor')
- grad_out_proj: float32 [2048, 2048], P('dp', 'tensor')
- grad_ln_gain: float32 [2, 2048], replicated
- grad_ln_bias: float32 [2, 2048], replicated
- grad_gate_up: float32 [2048, 2, 5632], P('dp', None, 'tensor')
- grad_down: float32 [2048, 5632], P('dp', 'tensor')
The draws below stay inside these ranges and needn't reach their ends.
All inputs are finite; a program needn't handle non-finite values.
Results may differ from the reference program's by a relative error of at most 0.023.
Values may be sent and summed in bfloat16 or wider, within the bound.
No kernel may reach another device: no remote copies, remote signals or barrier semaphores. Data moves between devices by JAX's collectives and lax.ppermute only.
A program may use at most 256 MiB of HBM per device.

```python
import math
import jax
import jax.numpy as jnp
from jax import lax

D = 2048
HEADS = 32
HEAD_DIM = 64
ROT = 16
FF = 5632
LEN = 1024
TOKENS = 8192


def with_spikes(entries, own_key, source, target, blocks, factor):
    def block_of(axis_at):
        return (jnp.arange(entries.shape[axis_at]) // (entries.shape[axis_at] // blocks)).reshape((-1,) + (1,) * (entries.ndim - 1 - axis_at))

    one_side = jax.random.permutation(own_key, blocks)[block_of(target)]
    second = (block_of(target) + blocks // 2) % blocks
    return jnp.where((block_of(source) == one_side) | (block_of(source) == second), factor * entries, entries)


def block_levels(own_key, dims, split, smallest, largest):
    level = 1.0
    for position, blocks in split:
        draws = jax.random.uniform(jax.random.fold_in(jax.random.fold_in(own_key, 6), position), (blocks,), jnp.float32, smallest / len(split), largest / len(split))
        level = level * jnp.repeat(jnp.exp(draws), dims[position] // blocks).reshape((-1,) + (1,) * (len(dims) - 1 - position))
    return level


def gaussian(key, extent, scale, reach, pieces=(), dtype=jnp.bfloat16):
    values = scale * jax.random.normal(key, extent, jnp.float32)
    if pieces:
        values = values * block_levels(key, extent, pieces, -0.22, 0.18)
    return jnp.clip(values, -reach, reach).astype(dtype)


def noise_with(rng, shape, scale, limit, shards, heavy, dtype=jnp.bfloat16):
    array = scale * jax.random.normal(rng, shape, jnp.float32)
    if shards:
        array = array * block_levels(rng, shape, shards, -0.22, 0.18)
    return jnp.clip(with_spikes(array, jax.random.fold_in(rng, 3), *heavy), -limit, limit).astype(dtype)


def setup_inputs(seed: int = 0) -> dict:
    arg_keys = jax.random.split(jax.random.key(seed), 11)
    hidden_in = gaussian(arg_keys[0], (TOKENS, D), 1.0, 6.0, ((0, 32),))
    w_qkv = gaussian(arg_keys[1], (D, 3, D), D ** -0.5, 0.125, ((0, 8), (2, 4)))
    qv_bias = gaussian(arg_keys[2], (2, D), 0.5, 3.0, ((1, 4),), jnp.float32)
    k_bias = gaussian(arg_keys[3], (HEADS, ROT), 0.5, 3.0, ((0, 4),), jnp.float32)
    w_out = gaussian(arg_keys[4], (D, D), (D // 64) ** -0.5, 1.0, ((0, 8), (1, 4)))
    ln_gain = jnp.clip(1.0 + 0.1 * jax.random.normal(arg_keys[5], (2, D), jnp.float32), 0.5, 1.5)
    ln_bias = gaussian(arg_keys[6], (2, D), 0.3, 1.75, (), jnp.float32)
    w_gate_up = gaussian(arg_keys[7], (D, 2, FF), D ** -0.5, 0.125, ((0, 8), (2, 4)))
    w_down = gaussian(arg_keys[8], (D, FF), FF ** -0.5, 0.078125, ((0, 8), (1, 4)))
    cotangent = noise_with(arg_keys[9], (TOKENS, D), 1.0, 12.0, ((0, 32),), (0, 1, 32, 2.75))
    return {"hidden_in": hidden_in, "w_qkv": w_qkv, "qv_bias": qv_bias, "k_bias": k_bias, "w_out": w_out, "ln_gain": ln_gain, "ln_bias": ln_bias, "w_gate_up": w_gate_up, "w_down": w_down, "cotangent": cotangent}


EPSILON = 1e-05

def normalize(values):
    centered = values - lax.optimization_barrier(jnp.mean(values, axis=-1, keepdims=True))
    inverse = lax.rsqrt(lax.optimization_barrier(jnp.mean(centered * centered, axis=-1, keepdims=True)) + EPSILON)
    return (centered * inverse, inverse)

def norm_back(upstream, gain, normed, inverse):
    scaled = upstream * gain
    return inverse * (scaled - lax.optimization_barrier(jnp.mean(scaled, axis=-1, keepdims=True)) - normed * lax.optimization_barrier(jnp.mean(scaled * normed, axis=-1, keepdims=True)))

def rotary_tables(count, seq_len, rotary):
    positions = (jnp.arange(count) % seq_len).astype(jnp.float32)
    freqs = 10000.0 ** (-(2.0 * jnp.arange(rotary // 2).astype(jnp.float32)) / rotary)
    angles = positions[:, None] * freqs[None, :]
    return (jnp.cos(angles)[:, None, :], jnp.sin(angles)[:, None, :])

def rotate(values, cosine, sine, rotary, direction):
    half = rotary // 2
    first = values[..., :half]
    second = values[..., half:rotary]
    return jnp.concatenate([first * cosine - direction * second * sine, second * cosine + direction * first * sine, values[..., rotary:]], axis=-1)

def reference(hidden_in, w_qkv, qv_bias, k_bias, w_out, ln_gain, ln_bias, w_gate_up, w_down, cotangent):
    seq_count = TOKENS // LEN
    scale = 1.0 / math.sqrt(HEAD_DIM)
    flat_qkv = w_qkv.reshape(D, 3 * D)
    flat_gate_up = w_gate_up.reshape(D, 2 * FF)
    cosine, sine = rotary_tables(LEN, LEN, ROT)
    key_shift = jnp.pad(k_bias, ((0, 0), (0, HEAD_DIM - ROT)))
    causal = jnp.arange(LEN)[:, None] >= jnp.arange(LEN)[None, :]

    def one_sequence(sums, inputs):
        rows, upstream = inputs
        residual = rows.astype(jnp.float32)
        normed1, inverse1 = normalize(residual)
        first_in = (normed1 * ln_gain[0] + ln_bias[0]).astype(jnp.bfloat16)
        projected = jnp.dot(first_in, flat_qkv, preferred_element_type=jnp.float32).reshape(LEN, 3, HEADS, HEAD_DIM)
        query = rotate(projected[:, 0] + qv_bias[0].reshape(HEADS, HEAD_DIM), cosine, sine, ROT, 1.0).astype(jnp.bfloat16)
        keys = rotate(projected[:, 1] + key_shift, cosine, sine, ROT, 1.0).astype(jnp.bfloat16)
        values = (projected[:, 2] + qv_bias[1].reshape(HEADS, HEAD_DIM)).astype(jnp.bfloat16)
        query_wide = query.astype(jnp.float32)
        keys_wide = keys.astype(jnp.float32)
        values_wide = values.astype(jnp.float32)
        scores = jnp.einsum('ihd,jhd->hij', query_wide, keys_wide) * scale
        masked = jnp.where(causal[None], scores, -1e+30)
        top = lax.optimization_barrier(jnp.max(masked, axis=-1, keepdims=True))
        lse = top + jnp.log(lax.optimization_barrier(jnp.sum(jnp.exp(masked - top), axis=-1, keepdims=True)))
        probs = jnp.exp(masked - lse).astype(jnp.bfloat16)
        probs_wide = probs.astype(jnp.float32)
        attended = jnp.einsum('hij,jhd->ihd', probs_wide, values_wide).astype(jnp.bfloat16).reshape(LEN, D)
        middle = residual + jnp.dot(attended, w_out.T, preferred_element_type=jnp.float32)
        normed2, inverse2 = normalize(middle)
        second_in = (normed2 * ln_gain[1] + ln_bias[1]).astype(jnp.bfloat16)
        gate_up = jnp.dot(second_in, flat_gate_up, preferred_element_type=jnp.float32).reshape(LEN, 2, FF)
        gate = gate_up[:, 0]
        upward = gate_up[:, 1]
        activated = jax.nn.silu(gate)
        hidden = (activated * upward).astype(jnp.bfloat16)
        layer_out = (middle + jnp.dot(hidden, w_down.T, preferred_element_type=jnp.float32)).astype(jnp.bfloat16)
        part_down = jnp.dot(upstream.T, hidden, preferred_element_type=jnp.float32)
        hidden_grad = jnp.dot(upstream, w_down, preferred_element_type=jnp.float32)
        sigmoid = jax.nn.sigmoid(gate)
        gate_up_grad = jnp.stack([hidden_grad * upward * sigmoid * (1.0 + gate * (1.0 - sigmoid)), hidden_grad * activated], axis=1).reshape(LEN, 2 * FF).astype(jnp.bfloat16)
        part_gate_up = jnp.dot(second_in.T, gate_up_grad, preferred_element_type=jnp.float32)
        second_grad = jnp.dot(gate_up_grad, flat_gate_up.T, preferred_element_type=jnp.float32)
        middle_grad = upstream.astype(jnp.float32) + norm_back(second_grad, ln_gain[1], normed2, inverse2)
        middle_low = middle_grad.astype(jnp.bfloat16)
        part_out = jnp.dot(middle_low.T, attended, preferred_element_type=jnp.float32)
        attended_grad = jnp.dot(middle_low, w_out, preferred_element_type=jnp.float32).astype(jnp.bfloat16)
        grad_heads = attended_grad.reshape(LEN, HEADS, HEAD_DIM).astype(jnp.float32)
        delta = lax.optimization_barrier(jnp.sum(grad_heads * attended.reshape(LEN, HEADS, HEAD_DIM).astype(jnp.float32), axis=-1))
        prob_grad = jnp.einsum('ihd,jhd->hij', grad_heads, values_wide)
        score_grad = (probs_wide * (prob_grad - delta.T[:, :, None])).astype(jnp.bfloat16).astype(jnp.float32)
        query_raw = jnp.einsum('hij,jhd->ihd', score_grad, keys_wide) * scale
        keys_raw = jnp.einsum('hij,ihd->jhd', score_grad, query_wide) * scale
        value_grad = jnp.einsum('hij,ihd->jhd', probs_wide, grad_heads)
        query_grad = rotate(query_raw, cosine, sine, ROT, -1.0)
        key_grad = rotate(keys_raw, cosine, sine, ROT, -1.0)
        part_qv = jnp.stack([lax.optimization_barrier(jnp.sum(query_grad, axis=0)).reshape(D), lax.optimization_barrier(jnp.sum(value_grad, axis=0)).reshape(D)])
        part_k = lax.optimization_barrier(jnp.sum(key_grad[..., :ROT], axis=0))
        proj_grad = jnp.stack([query_grad, key_grad, value_grad], axis=1).reshape(LEN, 3 * D).astype(jnp.bfloat16)
        part_qkv = jnp.dot(first_in.T, proj_grad, preferred_element_type=jnp.float32)
        first_grad = jnp.dot(proj_grad, flat_qkv.T, preferred_element_type=jnp.float32)
        grad_input = (middle_grad + norm_back(first_grad, ln_gain[0], normed1, inverse1)).astype(jnp.bfloat16)
        part_gain = jnp.stack([lax.optimization_barrier(jnp.sum(first_grad * normed1, axis=0)), lax.optimization_barrier(jnp.sum(second_grad * normed2, axis=0))])
        part_bias = jnp.stack([lax.optimization_barrier(jnp.sum(first_grad, axis=0)), lax.optimization_barrier(jnp.sum(second_grad, axis=0))])
        parts = (part_qkv, part_qv, part_k, part_out, part_gain, part_bias, part_gate_up, part_down)
        new_sums = tuple((total + piece for total, piece in zip(sums, parts)))
        return (new_sums, (layer_out, grad_input))
    start = (jnp.zeros((D, 3 * D), jnp.float32), jnp.zeros((2, D), jnp.float32), jnp.zeros((HEADS, ROT), jnp.float32), jnp.zeros((D, D), jnp.float32), jnp.zeros((2, D), jnp.float32), jnp.zeros((2, D), jnp.float32), jnp.zeros((D, 2 * FF), jnp.float32), jnp.zeros((D, FF), jnp.float32))
    sequences = (hidden_in.reshape(seq_count, LEN, D), cotangent.reshape(seq_count, LEN, D))
    sums, results = lax.scan(one_sequence, start, sequences)
    layer_out = results[0].reshape(TOKENS, D)
    grad_input = results[1].reshape(TOKENS, D)
    return (layer_out, grad_input, sums[0].reshape(D, 3, D), sums[1], sums[2], sums[3], sums[4], sums[5], sums[6].reshape(D, 2, FF), sums[7])
```

```python
import functools
import jax, jax.numpy as jnp
from jax import lax
from jax.experimental import pallas as pl
from jax.experimental.pallas import tpu as pltpu
from jax.sharding import PartitionSpec as P

LANES = 128
HEAD = 64
LEN = 1024
EPSILON = 1e-05


def lane_partner(values, half):
    lane = lax.broadcasted_iota(jnp.int32, values.shape, 1) % HEAD
    ahead = pltpu.roll(values, LANES - half, 1)
    behind = pltpu.roll(values, half, 1)
    return jnp.where(lane < half, ahead, behind)


def forward_kernel(
    count, rows, half, scale, block_of,
    raw_q, raw_k, raw_v, cosine, sine, bias_q, bias_k, bias_v,
    query, keys, values, attended, lse_out,
):
    for slot in range(count):
        source = pl.ds(slot * rows, rows)
        target = pl.ds(pl.multiple_of(block_of[slot] * rows, rows), rows)
        cos_part = cosine[source, :]
        sin_part = sine[source, :]
        wide_q = raw_q[source, :] + bias_q[...]
        wide_k = raw_k[source, :] + bias_k[...]
        wide_q = wide_q * cos_part + lane_partner(wide_q, half) * sin_part
        wide_k = wide_k * cos_part + lane_partner(wide_k, half) * sin_part
        query[target, :] = wide_q.astype(jnp.bfloat16) * scale
        keys[target, :] = wide_k.astype(jnp.bfloat16)
        values[target, :] = (raw_v[source, :] + bias_v[...]).astype(jnp.bfloat16)
    lane = lax.broadcasted_iota(jnp.int32, (rows, LANES), 1)
    first_head = lane < HEAD
    below = lax.broadcasted_iota(jnp.int32, (rows, rows), 0) >= lax.broadcasted_iota(
        jnp.int32, (rows, rows), 1
    )
    for block in range(count):
        span = (block + 1) * rows
        tile = query[block * rows : span, :]
        outs = []
        sums = []
        for head in range(2):
            mine = first_head if head == 0 else jnp.logical_not(first_head)
            masked_tile = jnp.where(mine, tile, jnp.zeros_like(tile))
            pieces = []
            for part in range(block + 1):
                piece = lax.dot_general(
                    masked_tile,
                    keys[part * rows : (part + 1) * rows, :],
                    (((1,), (1,)), ((), ())),
                    preferred_element_type=jnp.float32,
                )
                if part == block:
                    piece = jnp.where(below, piece, -1e30)
                pieces.append(piece)
            top = functools.reduce(jnp.maximum, pieces)
            top = jnp.max(top, axis=1, keepdims=True)
            total = None
            mixed = None
            for part in range(block + 1):
                weight = jnp.exp(pieces[part] - top)
                term = jnp.dot(
                    weight.astype(jnp.bfloat16),
                    values[part * rows : (part + 1) * rows, :],
                    preferred_element_type=jnp.float32,
                )
                total = weight if total is None else total + weight
                mixed = term if mixed is None else mixed + term
            total = jnp.sum(total, axis=1, keepdims=True)
            outs.append(mixed / total)
            sums.append(top + jnp.log(total))
        slot_rows = pl.ds(pl.multiple_of(block_of[block] * rows, rows), rows)
        attended[slot_rows, :] = jnp.where(first_head, outs[0], outs[1]).astype(jnp.bfloat16)
        lse_out[block * rows : span, :] = jnp.where(first_head, sums[0], sums[1])


def attention_forward(block_of, projected, cosine, sine, bias, count, half):
    total = projected.shape[0]
    width = projected.shape[1] // 3
    pairs = width // LANES
    rows = total // count
    column = lambda offset: pl.BlockSpec((total, LANES), lambda pair, ref: (0, pair + offset))
    shift = lambda offset: pl.BlockSpec((1, LANES), lambda pair, ref: (0, pair + offset))
    table = pl.BlockSpec((total, LANES), lambda pair, ref: (0, 0))
    narrow = jax.ShapeDtypeStruct((total, width), jnp.bfloat16)
    return pl.pallas_call(
        functools.partial(forward_kernel, count, rows, half, HEAD**-0.5),
        out_shape=(narrow, narrow, narrow, narrow, jax.ShapeDtypeStruct((total, width), jnp.float32)),
        grid_spec=pltpu.PrefetchScalarGridSpec(
            num_scalar_prefetch=1,
            grid=(pairs,),
            in_specs=[
                column(0), column(pairs), column(2 * pairs), table, table,
                shift(0), shift(pairs), shift(2 * pairs),
            ],
            out_specs=[column(0)] * 5,
        ),
        cost_estimate=pl.CostEstimate(
            flops=8 * total * total * width, bytes_accessed=total * width * 28,
            transcendentals=total * total * width // 128,
        ),
        name="attention_forward",
    )(block_of, projected, projected, projected, cosine, sine, bias, bias, bias)


def backward_kernel(
    count, rows, half, scale, block_of,
    query, keys, values, attended, upstream, lse_in, cosine, sine,
    grads, sums,
    ordered_up, product, key_grad, value_grad,
):
    pair = pl.program_id(0)
    pairs = pl.num_programs(0)
    total = count * rows
    for slot in range(count):
        source = pl.ds(slot * rows, rows)
        target = pl.ds(pl.multiple_of(block_of[slot] * rows, rows), rows)
        up_part = upstream[source, :]
        ordered_up[target, :] = up_part
        product[target, :] = up_part.astype(jnp.float32) * attended[source, :].astype(jnp.float32)
    across = product[...].T
    deltas = [jnp.sum(across[:HEAD], axis=0, keepdims=True), jnp.sum(across[HEAD:], axis=0, keepdims=True)]
    lse_across = lse_in[...].T
    lses = [lse_across[0:1], lse_across[HEAD : HEAD + 1]]
    keys_across = keys[...].T
    first_head = lax.broadcasted_iota(jnp.int32, (rows, LANES), 1) < HEAD
    upper_rows = lax.broadcasted_iota(jnp.int32, (LANES, rows), 0) < HEAD
    above = lax.broadcasted_iota(jnp.int32, (rows, rows), 0) <= lax.broadcasted_iota(
        jnp.int32, (rows, rows), 1
    )

    def finish(which, block, grad, rotated):
        slot = block_of[block]
        slot_rows = pl.ds(pl.multiple_of(slot * rows, rows), rows)
        if rotated:
            grad = grad * cosine[slot_rows, :] - lane_partner(grad, half) * sine[slot_rows, :]
        columns = pl.ds(pl.multiple_of((which * pairs + pair) * LANES, LANES), LANES)
        grads[slot_rows, columns] = grad.astype(jnp.bfloat16)
        return jnp.sum(grad, axis=0, keepdims=True), columns

    query_sum = None
    for block in reversed(range(count)):
        span = slice(block * rows, (block + 1) * rows)
        tile = query[span, :]
        up_tile = ordered_up[span, :]
        query_across = []
        for head in range(2):
            mine = first_head if head == 0 else jnp.logical_not(first_head)
            masked_tile = jnp.where(mine, tile, jnp.zeros_like(tile))
            masked_up = jnp.where(mine, up_tile, jnp.zeros_like(up_tile))
            grad_across = None
            for part in range(block + 1):
                part_rows = slice(part * rows, (part + 1) * rows)
                scores = lax.dot_general(
                    keys[part_rows, :], masked_tile, (((1,), (1,)), ((), ())),
                    preferred_element_type=jnp.float32,
                )
                if part == block:
                    scores = jnp.where(above, scores, -1e30)
                probs = jnp.exp(scores - lses[head][:, span])
                prob_grad = lax.dot_general(
                    values[part_rows, :], masked_up, (((1,), (1,)), ((), ())),
                    preferred_element_type=jnp.float32,
                )
                score_grad = (probs * (prob_grad - deltas[head][:, span])).astype(jnp.bfloat16)
                value_term = jnp.dot(
                    probs.astype(jnp.bfloat16), masked_up, preferred_element_type=jnp.float32
                )
                key_term = jnp.dot(score_grad, masked_tile, preferred_element_type=jnp.float32)
                if block == count - 1 and head == 0:
                    value_grad[part_rows, :] = value_term
                    key_grad[part_rows, :] = key_term
                else:
                    value_grad[part_rows, :] += value_term
                    key_grad[part_rows, :] += key_term
                term = jnp.dot(
                    keys_across[:, part_rows], score_grad, preferred_element_type=jnp.float32
                )
                grad_across = term if grad_across is None else grad_across + term
            query_across.append(grad_across)
        query_grad = jnp.where(upper_rows, query_across[0], query_across[1]).T * scale
        part_sum, columns = finish(0, block, query_grad, True)
        query_sum = part_sum if query_sum is None else query_sum + part_sum
    sums[:, columns] = query_sum
    key_sum = None
    value_sum = None
    for block in range(count):
        span = slice(block * rows, (block + 1) * rows)
        part_sum, key_columns = finish(1, block, key_grad[span, :], True)
        key_sum = part_sum if key_sum is None else key_sum + part_sum
        part_sum, value_columns = finish(2, block, value_grad[span, :], False)
        value_sum = part_sum if value_sum is None else value_sum + part_sum
    sums[:, key_columns] = key_sum
    sums[:, value_columns] = value_sum


def attention_backward(block_of, query, keys, values, attended, upstream, lse, cosine, sine, count, half):
    total, width = query.shape
    pairs = width // LANES
    rows = total // count
    column = pl.BlockSpec((total, LANES), lambda pair, ref: (0, pair))
    table = pl.BlockSpec((total, LANES), lambda pair, ref: (0, 0))
    whole = lambda extent: pl.BlockSpec(extent, lambda pair, ref: (0, 0))
    return pl.pallas_call(
        functools.partial(backward_kernel, count, rows, half, HEAD**-0.5),
        out_shape=(
            jax.ShapeDtypeStruct((total, 3 * width), jnp.bfloat16),
            jax.ShapeDtypeStruct((1, 3 * width), jnp.float32),
        ),
        grid_spec=pltpu.PrefetchScalarGridSpec(
            num_scalar_prefetch=1,
            grid=(pairs,),
            in_specs=[column] * 6 + [table] * 2,
            out_specs=[whole((total, 3 * width)), whole((1, 3 * width))],
            scratch_shapes=[
                pltpu.VMEM((total, LANES), jnp.bfloat16),
                pltpu.VMEM((total, LANES), jnp.float32),
                pltpu.VMEM((total, LANES), jnp.float32),
                pltpu.VMEM((total, LANES), jnp.float32),
            ],
        ),
        cost_estimate=pl.CostEstimate(
            flops=20 * total * total * width, bytes_accessed=total * width * 20,
            transcendentals=total * total * width // 128,
        ),
        name="attention_backward",
    )(block_of, query, keys, values, attended, upstream, lse, cosine, sine)


def rope_tables(block_of, count, rows, rotary):
    half = rotary // 2
    lane = jnp.arange(LANES) % HEAD
    index = (lane % half).astype(jnp.float32)
    freqs = 10000.0 ** (-(2.0 * index) / rotary)
    rotated = lane < rotary
    local = jnp.arange(rows)
    positions = (block_of[:, None] * rows + local[None, :]).reshape(-1).astype(jnp.float32)
    angles = jnp.where(rotated[None, :], positions[:, None] * freqs[None, :], 0.0)
    sign = jnp.where(lane < half, -1.0, 1.0)
    return jnp.cos(angles), jnp.sin(angles) * sign[None, :]


def normalize(values):
    centered = values - jnp.mean(values, axis=-1, keepdims=True)
    inverse = lax.rsqrt(jnp.mean(centered * centered, axis=-1, keepdims=True) + EPSILON)
    return (centered * inverse, inverse)


def norm_back(upstream, gain, normed, inverse):
    scaled = upstream * gain
    return inverse * (
        scaled
        - jnp.mean(scaled, axis=-1, keepdims=True)
        - normed * jnp.mean(scaled * normed, axis=-1, keepdims=True)
    )


def shift(values, axis, amount):
    size = lax.axis_size(axis)
    return lax.ppermute(values, axis, [(at, (at + amount) % size) for at in range(size)])


def dot_rows(left, right):
    return lax.dot_general(left, right, (((1,), (1,)), ((), ())), preferred_element_type=jnp.float32)


def dot_tokens(left, right):
    return lax.dot_general(left, right, (((0,), (0,)), ((), ())), preferred_element_type=jnp.float32)


def dot_plain(left, right):
    return jnp.dot(left, right, preferred_element_type=jnp.float32)


def ring_gather(values, axis):
    held = [values]
    for _ in range(lax.axis_size(axis) - 1):
        held.append(shift(held[-1], axis, 1))
    return held


def ring_sum(part_of, axis):
    count = lax.axis_size(axis)
    moving = part_of(1)
    for slot in range(2, count + 1):
        moving = moving.astype(jnp.bfloat16)
        moving = shift(moving, axis, 1).astype(jnp.float32) + part_of(slot % count)
    return moving


def gather_dp(weight):
    return lax.all_gather(weight, "dp", axis=0, tiled=True)


def scatter_dp(grad):
    return lax.psum_scatter(grad, "dp", scatter_dimension=0, tiled=True)


def sum_over(values, axis):
    step = 1
    size = lax.axis_size(axis)
    while step < size:
        values = values + lax.ppermute(values, axis, [(at, at ^ step) for at in range(size)])
        step *= 2
    return values


def body(hidden_in, w_qkv, qv_bias, k_bias, w_out, ln_gain, ln_bias, w_gate_up, w_down, cotangent):
    count = lax.axis_size("tensor")
    rows, width = hidden_in.shape
    weight_rows = w_qkv.shape[0]
    local_heads, rotary = k_bias.shape
    local_width = qv_bias.shape[1]
    units = w_down.shape[1]
    assert rows * count == LEN and local_width == local_heads * HEAD
    slots = range(count)
    here = lax.axis_index("tensor")
    block_of = ((here - jnp.arange(count)) % count).astype(jnp.int32)
    cosine, sine = rope_tables(block_of, count, rows, rotary)
    key_shift = jnp.pad(k_bias, ((0, 0), (0, HEAD - rotary))).reshape(local_width)
    bias = jnp.concatenate([qv_bias[0], key_shift, qv_bias[1]])[None]

    residual = hidden_in.astype(jnp.float32)
    normed1, inverse1 = normalize(residual)
    first_slots = ring_gather((normed1 * ln_gain[0] + ln_bias[0]).astype(jnp.bfloat16), "tensor")
    all_qkv = gather_dp(w_qkv.reshape(weight_rows, 3 * local_width))
    out_slots = jnp.concatenate([shift(w_out, "tensor", -slot) if slot else w_out for slot in slots], axis=1)
    all_gate_up = gather_dp(w_gate_up.reshape(weight_rows, 2 * units))
    all_out = gather_dp(out_slots)
    all_down = gather_dp(w_down)

    projected = jnp.concatenate([dot_plain(part, all_qkv) for part in first_slots], axis=0)
    query, keys, values, attended, lse = attention_forward(
        block_of, projected, cosine, sine, bias, count, rotary // 2
    )
    mine = jnp.concatenate(
        [
            shift(attended[slot * rows : (slot + 1) * rows], "tensor", -slot) if slot else attended[:rows]
            for slot in slots
        ],
        axis=1,
    )
    middle = residual + dot_rows(mine, all_out)
    normed2, inverse2 = normalize(middle)
    cot_slots = ring_gather(cotangent, "tensor")
    second_slots = ring_gather((normed2 * ln_gain[1] + ln_bias[1]).astype(jnp.bfloat16), "tensor")

    hidden_slots = [None] * count
    gate_up_grads = [None] * count
    second_parts = [None] * count
    for slot in slots:
        gate = dot_plain(second_slots[slot], all_gate_up[:, :units])
        upward = dot_plain(second_slots[slot], all_gate_up[:, units:])
        hidden_grad = dot_plain(cot_slots[slot], all_down)
        sigmoid = jax.nn.sigmoid(gate)
        activated = gate * sigmoid
        hidden_slots[slot] = (activated * upward).astype(jnp.bfloat16)
        gate_up_grads[slot] = jnp.concatenate(
            [
                (hidden_grad * upward * sigmoid * (1.0 + gate * (1.0 - sigmoid))).astype(jnp.bfloat16),
                (hidden_grad * activated).astype(jnp.bfloat16),
            ],
            axis=1,
        )
        second_parts[slot] = dot_rows(gate_up_grads[slot], all_gate_up)
    second_grad = ring_sum(lambda slot: second_parts[slot], "tensor")
    second_rows = jnp.concatenate(second_slots, axis=0)
    cot_rows = jnp.concatenate(cot_slots, axis=0)
    hidden = jnp.concatenate(hidden_slots, axis=0)
    gate_up_grad = jnp.concatenate(gate_up_grads, axis=0)
    grad_down = scatter_dp(dot_tokens(cot_rows, hidden).astype(jnp.bfloat16))
    grad_gate_up = scatter_dp(dot_tokens(second_rows, gate_up_grad).astype(jnp.bfloat16))
    down = ring_sum(lambda slot: dot_rows(hidden_slots[slot], all_down), "tensor")
    layer_out = (middle + down).astype(jnp.bfloat16)

    middle_grad = cotangent.astype(jnp.float32) + norm_back(second_grad, ln_gain[1], normed2, inverse2)
    middle_low = middle_grad.astype(jnp.bfloat16)
    mine_grad = dot_plain(middle_low, all_out).astype(jnp.bfloat16)
    attended_grad = jnp.concatenate(
        [
            shift(mine_grad[:, slot * local_width : (slot + 1) * local_width], "tensor", slot)
            if slot
            else mine_grad[:, :local_width]
            for slot in slots
        ],
        axis=0,
    )
    grad_out_wide = scatter_dp(dot_tokens(middle_low, mine).astype(jnp.bfloat16))
    grad_out = grad_out_wide[:, :local_width].astype(jnp.float32)
    for slot in range(1, count):
        moved = shift(grad_out_wide[:, slot * local_width : (slot + 1) * local_width], "tensor", slot)
        grad_out = grad_out + moved.astype(jnp.float32)
    proj_grad, proj_sums = attention_backward(
        block_of, query, keys, values, attended, attended_grad, lse, cosine, sine, count, rotary // 2
    )
    first_grad = ring_sum(
        lambda slot: dot_rows(proj_grad[slot * rows : (slot + 1) * rows], all_qkv), "tensor"
    )
    first_rows = jnp.concatenate(first_slots, axis=0)
    grad_qkv = scatter_dp(dot_tokens(first_rows, proj_grad).astype(jnp.bfloat16))
    grad_input = (middle_grad + norm_back(first_grad, ln_gain[0], normed1, inverse1)).astype(jnp.bfloat16)

    proj_sums = sum_over(proj_sums, "dp").reshape(3, local_width)
    grad_qv_bias = proj_sums[::2]
    grad_k_bias = proj_sums[1].reshape(local_heads, HEAD)[:, :rotary]
    norm_sums = [
        sum_over(
            sum_over(
                jnp.stack([jnp.sum(grad * normed, axis=0), jnp.sum(grad, axis=0)]), "dp"
            ),
            "tensor",
        )
        for grad, normed in ((first_grad, normed1), (second_grad, normed2))
    ]
    return (
        layer_out,
        grad_input,
        grad_qkv.astype(jnp.float32).reshape(weight_rows, 3, local_width),
        grad_qv_bias,
        grad_k_bias,
        grad_out,
        jnp.stack([norm_sums[0][0], norm_sums[1][0]]),
        jnp.stack([norm_sums[0][1], norm_sums[1][1]]),
        grad_gate_up.astype(jnp.float32).reshape(weight_rows, 2, units),
        grad_down.astype(jnp.float32),
    )


def solution(mesh):
    placed = (
        P(("dp", "tensor"), None),
        P("dp", None, "tensor"),
        P(None, "tensor"),
        P("tensor", None),
        P("dp", "tensor"),
        P(),
        P(),
        P("dp", None, "tensor"),
        P("dp", "tensor"),
        P(("dp", "tensor"), None),
    )
    return jax.shard_map(
        body,
        mesh=mesh,
        in_specs=placed,
        out_specs=(
            P(("dp", "tensor"), None),
            P(("dp", "tensor"), None),
            P("dp", None, "tensor"),
            P(None, "tensor"),
            P("tensor", None),
            P("dp", "tensor"),
            P(),
            P(),
            P("dp", None, "tensor"),
            P("dp", "tensor"),
        ),
        check_vma=False,
    )
```
